32 devices in a mesh: ep: 16 (over z, x, core), fs: 2 (over y).
Axes of the slice: x: 2, y: 2, z: 4, core: 2. Of those that a mesh axis runs over, the one named last changes fastest.
Arguments:
- tokens: bfloat16 [2048, 4096], P('ep', 'fs'), may hold values from -6 to 6
- cotangent: bfloat16 [2048, 4096], P('ep', 'fs'), may hold values from -3 to 3
- gate_probs: bfloat16 [2048, 8], P('ep'), may hold values from 0.019897461 to 0.3984375
- expert_ids: int32 [2048, 8], P('ep'), may hold values from 0 to 15, all different within a row; in each aligned block of 128 rows (0 to 127, 128 to 255, ...) at most 72 rows name the same one
- w_gate: bfloat16 [16, 4096, 768], P('ep', 'fs'), may hold values from -0.09375 to 0.09375
- w_up: bfloat16 [16, 4096, 768], P('ep', 'fs'), may hold values from -0.09375 to 0.09375
- w_down: bfloat16 [16, 768, 4096], P('ep', None, 'fs'), may hold values from -0.21875 to 0.21875
Outputs:
- grad_tokens: bfloat16 [2048, 4096], P('ep', 'fs')
- grad_probs: bfloat16 [2048, 8], P('ep')
- grad_w_gate: bfloat16 [16, 4096, 768], P('ep', 'fs')
- grad_w_up: bfloat16 [16, 4096, 768], P('ep', 'fs')
- grad_w_down: bfloat16 [16, 768, 4096], P('ep', None, 'fs')
The draws below stay inside these ranges and needn't reach their ends.
Inputs may be any that keep to these rules, and one draw needn't show every extreme that they name: `expert_ids`: each token names 8 different experts. Among the 128 tokens of one index of ep, no expert is named by more than 72 of them, and in every draw some expert is named by exactly 72.
All inputs are finite; a program needn't handle non-finite values.
Results may differ from the reference program's by a relative error of at most 0.025.
Values may be sent and summed in bfloat16 or wider, within the bound.
A program may use at most 128 MiB of HBM per device.

```python
import math
import jax
import jax.numpy as jnp
import numpy as np
from jax import lax

D = 4096
FF = 768
TOP = 8
TOK_DEV = 128
EXPERTS = 16
TOKENS = 2048
CAP = 72
N_FS = 2


def steps_of(rng, dims, split, low, top_value):
    def one(axis_at, parts):
        steps = jax.random.uniform(jax.random.fold_in(jax.random.fold_in(rng, 6), axis_at), (parts,), jnp.float32, low / len(split), top_value / len(split))
        return jnp.repeat(jnp.exp(steps), dims[axis_at] // parts).reshape((-1,) + (1,) * (len(dims) - axis_at - 1))

    level = one(*split[0])
    for cut in split[1:]:
        level = level * one(*cut)
    return level


def deal_out(own_key, own, number, rows, count, top, limit, lean):
    ranking = jax.random.permutation(own_key, count)
    heavy_load, usual = shares(count, rows * top, limit, lean, True), shares(count, rows * top, limit, lean, False)
    places = jnp.arange(count)

    def named(tallies, rotation):
        used = int((tallies > 0).sum())
        fixed = max(1, used // 4)
        passed = fixed + (places - fixed + rotation * (used - fixed)) % max(1, count - fixed)
        return jnp.zeros((count,), jnp.int32).at[ranking[jnp.where(places < fixed, places, passed)]].set(jnp.asarray(tallies, jnp.int32))

    tallies = jnp.where(number % 4 == 0, named(heavy_load, number // 4), named(usual, number - number // 4 - 1))
    mixed = jax.random.permutation(jax.random.fold_in(own, 3), count)
    donor, receiver = mixed[0:count // 2 * 2:2], mixed[1:count // 2 * 2:2]
    margin = jnp.minimum(tallies[donor] - 1, limit - tallies[receiver]) // 2
    margin = jnp.where((donor == ranking[0]) | (receiver == ranking[0]) | (tallies[receiver] == 0), 0, jnp.maximum(margin, 0))
    passed = jax.random.randint(jax.random.fold_in(own, 4), (count // 2,), 0, 1 << 20) % (margin + 1)
    tallies = tallies.at[donor].add(-passed).at[receiver].add(passed)
    items = jnp.searchsorted(jnp.cumsum(tallies), jnp.arange(rows * top), side="right").astype(jnp.int32)
    table = items.reshape(top, rows).T
    table = table[jax.random.permutation(jax.random.fold_in(own, 1), rows)]
    rotation = jax.random.randint(jax.random.fold_in(own, 2), (rows, 1), 0, top)
    return jnp.take_along_axis(table, (jnp.arange(top)[None, :] + rotation) % top, axis=1)


def shares(number_of, total, bound, skew, full):
    portions = [(1 << 20) // math.isqrt(standing ** skew) + 1 for standing in range(1, number_of + 1)]
    largest = bound if full else min(bound, max(-(-total // number_of), total * portions[0] // sum(portions)))
    least = 1 if total - largest >= number_of - 1 else 0
    given, rest = [largest] + [least] * (number_of - 1), total - largest - least * (number_of - 1)
    while rest > 0:
        movable = [i for i in range(1, number_of) if given[i] < largest] or [i for i in range(1, number_of) if given[i] < bound]
        pool, budget = sum([portions[i] for i in movable]), rest
        for i in movable:
            addition = min(bound - given[i], max(1, budget * portions[i] // pool), rest)
            given[i] = given[i] + addition
            rest = rest - addition
    return np.array(given)


def centred(key, shape, deviation, most, shards=(), kind=jnp.bfloat16):
    level = steps_of(key, shape, shards, -0.22, 0.18) if shards else 1.0
    entries = jax.random.normal(key, shape, jnp.float32) * deviation * level
    return jnp.minimum(jnp.maximum(entries, -most), most).astype(kind)


def setup_inputs(seed: int = 0) -> dict:
    streams_of = jax.random.split(jax.random.key(seed), 8)
    tokens = centred(streams_of[0], (TOKENS, D), 1.0, 6.0, ((0, 16), (1, 2)))
    cotangent = centred(streams_of[1], (TOKENS, D), 0.5, 3.0, ((0, 16), (1, 2)))
    gate_probs = jnp.clip(jnp.exp(math.log(0.3984375) - 2.9969585 * jax.random.uniform(streams_of[2], (TOKENS, TOP), jnp.float32) ** steps_of(streams_of[2], (TOKENS, TOP), ((0, 16),), -0.2, 0.2)), 0.019897461, 0.3984375).astype(jnp.bfloat16)
    expert_ids_keys = jax.random.split(jax.random.fold_in(streams_of[3], 1), TOKENS // TOK_DEV)
    expert_ids_turns = jax.random.permutation(jax.random.fold_in(streams_of[3], 3), TOKENS // TOK_DEV)
    expert_ids = jax.vmap(lambda own, number: deal_out(jax.random.fold_in(streams_of[3], 2), own, number, TOK_DEV, EXPERTS, TOP, CAP, 1))(expert_ids_keys, expert_ids_turns).reshape((TOKENS, TOP))
    w_gate = centred(streams_of[4], (EXPERTS, D, FF), D ** -0.5, 0.09375, ((0, 16), (1, 2)))
    w_up = centred(streams_of[5], (EXPERTS, D, FF), D ** -0.5, 0.09375, ((0, 16), (1, 2)))
    w_down = centred(streams_of[6], (EXPERTS, FF, D), FF ** -0.5, 0.21875, ((0, 16), (2, 2)))
    return {"tokens": tokens, "cotangent": cotangent, "gate_probs": gate_probs, "expert_ids": expert_ids, "w_gate": w_gate, "w_up": w_up, "w_down": w_down}


def build_slots(routing, experts, capacity):
    flat_ids = routing.reshape(-1).astype(jnp.int32)
    choose = (flat_ids[:, None] == jnp.arange(experts, dtype=jnp.int32)[None, :]).astype(jnp.int32)
    earlier = jnp.cumsum(choose, axis=0) - choose
    position = jnp.sum(earlier * choose, axis=1).astype(jnp.int32)
    slot_of = (flat_ids * capacity + position).astype(jnp.int32)
    pair_number = jnp.arange(flat_ids.shape[0], dtype=jnp.int32) + 1
    filled_by = jnp.zeros((experts * capacity,), jnp.int32).at[slot_of].set(pair_number)
    return slot_of, filled_by


def blocked_sum(product_blocks):
    rounded = lax.optimization_barrier(product_blocks.astype(jnp.bfloat16))
    return jnp.sum(rounded.astype(jnp.float32), axis=1)


def reference(tokens, cotangent, gate_probs, expert_ids, w_gate, w_up, w_down):
    sources = TOKENS // TOK_DEV
    width_block = D // N_FS
    slot_count = sources * CAP
    blocks = expert_ids.reshape(sources, TOK_DEV * TOP)
    slot_of, filled_by = jax.vmap(lambda routing: build_slots(routing, EXPERTS, CAP))(blocks)
    per_expert = filled_by.reshape(sources, EXPERTS, CAP).transpose(1, 0, 2).reshape(EXPERTS, slot_count)
    source_row = jnp.repeat(jnp.arange(sources, dtype=jnp.int32), CAP)
    flat_probs = gate_probs.reshape(-1)

    def expert_step(carry, inputs):
        grad_acc, prob_acc = carry
        filled_row, gate_weight, up_weight, down_weight = inputs
        filled = filled_row > 0
        assign = jnp.maximum(filled_row - 1, 0).astype(jnp.int32)
        token_index = (source_row * TOK_DEV + assign // TOP).astype(jnp.int32)
        pair_index = (token_index * TOP + assign % TOP).astype(jnp.int32)
        token_rows = jnp.where(filled[:, None], tokens[token_index], jnp.zeros((), tokens.dtype))
        grad_rows = jnp.where(filled[:, None], cotangent[token_index], jnp.zeros((), cotangent.dtype))
        prob_rows = jnp.where(filled, flat_probs[pair_index], jnp.zeros((), gate_probs.dtype)).astype(jnp.float32)
        token_blocks = token_rows.astype(jnp.float32).reshape(slot_count, N_FS, width_block)
        gate_blocks = jnp.einsum("snf,nfh->snh", token_blocks, gate_weight.astype(jnp.float32).reshape(N_FS, width_block, FF))
        up_blocks = jnp.einsum("snf,nfh->snh", token_blocks, up_weight.astype(jnp.float32).reshape(N_FS, width_block, FF))
        gate_proj = lax.optimization_barrier(blocked_sum(gate_blocks).astype(jnp.bfloat16)).astype(jnp.float32)
        up_proj = lax.optimization_barrier(blocked_sum(up_blocks).astype(jnp.bfloat16)).astype(jnp.float32)
        sigmoid_gate = jax.nn.sigmoid(gate_proj)
        gate_act = gate_proj * sigmoid_gate
        hidden = (gate_act * up_proj).astype(jnp.bfloat16)
        grad_blocks = grad_rows.astype(jnp.float32).reshape(slot_count, N_FS, width_block)
        down_blocks = jnp.einsum("snf,hnf->snh", grad_blocks, down_weight.astype(jnp.float32).reshape(FF, N_FS, width_block))
        raw_grad = blocked_sum(down_blocks)
        grad_prob = jnp.sum(hidden.astype(jnp.float32) * raw_grad, axis=1).astype(jnp.bfloat16)
        scaled = prob_rows[:, None] * raw_grad
        grad_gate = (scaled * up_proj * sigmoid_gate * (1.0 + gate_proj * (1.0 - sigmoid_gate))).astype(jnp.bfloat16)
        grad_up = (scaled * gate_act).astype(jnp.bfloat16)
        weighted = (prob_rows[:, None] * grad_rows.astype(jnp.float32)).astype(jnp.bfloat16)
        new_gate = jnp.dot(token_rows.T, grad_gate, preferred_element_type=jnp.float32).astype(jnp.bfloat16)
        new_up = jnp.dot(token_rows.T, grad_up, preferred_element_type=jnp.float32).astype(jnp.bfloat16)
        new_down = jnp.dot(hidden.T, weighted, preferred_element_type=jnp.float32).astype(jnp.bfloat16)
        grad_part = (jnp.dot(grad_gate, gate_weight.T, preferred_element_type=jnp.float32)
                     + jnp.dot(grad_up, up_weight.T, preferred_element_type=jnp.float32)).astype(jnp.bfloat16)
        target = jnp.where(filled, token_index, TOKENS).astype(jnp.int32)
        grad_acc = grad_acc.at[target].add(grad_part.astype(jnp.float32), mode="drop")
        pair_target = jnp.where(filled, pair_index, TOKENS * TOP).astype(jnp.int32)
        prob_acc = prob_acc.at[pair_target].add(grad_prob.astype(jnp.float32), mode="drop")
        return (grad_acc, prob_acc), (new_gate, new_up, new_down)

    start_state = (jnp.zeros((TOKENS, D), jnp.float32), jnp.zeros((TOKENS * TOP,), jnp.float32))
    final_state, weight_grads = lax.scan(expert_step, start_state, (per_expert, w_gate, w_up, w_down))
    grad_acc, prob_acc = final_state
    grad_w_gate, grad_w_up, grad_w_down = weight_grads
    return (grad_acc.astype(jnp.bfloat16), prob_acc.reshape(TOKENS, TOP).astype(jnp.bfloat16),
            grad_w_gate, grad_w_up, grad_w_down)
```

```python
import jax
import jax.numpy as jnp
from jax import lax
from jax.sharding import PartitionSpec as P


def build_slots(routing, experts, capacity):
    flat_ids = routing.reshape(-1)
    choose = (flat_ids[:, None] == jnp.arange(experts, dtype=jnp.int32)[None, :]).astype(jnp.int32)
    earlier = jnp.cumsum(choose, axis=0) - choose
    position = jnp.sum(earlier * choose, axis=1)
    slot_of = flat_ids * capacity + position
    pair_number = jnp.arange(flat_ids.shape[0], dtype=jnp.int32) + 1
    filled_by = jnp.zeros((experts * capacity,), jnp.int32).at[slot_of].set(pair_number)
    return (slot_of, filled_by)


def activate(gate_up, hidden_units):
    gate_proj = gate_up[:, :hidden_units].astype(jnp.float32)
    up_proj = gate_up[:, hidden_units:].astype(jnp.float32)
    sigmoid_gate = jax.nn.sigmoid(gate_proj)
    gate_act = gate_proj * sigmoid_gate
    return (gate_proj, up_proj, sigmoid_gate, gate_act)


def local_grads(raw_grad, gate_up, prob_rows, hidden_units):
    gate_proj, up_proj, sigmoid_gate, gate_act = activate(gate_up, hidden_units)
    hidden = (gate_act * up_proj).astype(jnp.bfloat16)
    scaled = prob_rows.astype(jnp.float32)[:, None] * raw_grad
    grad_gate = scaled * up_proj * sigmoid_gate * (1.0 + gate_proj * (1.0 - sigmoid_gate))
    grad_up = scaled * gate_act
    grad_gate_up = jnp.concatenate(
        [grad_gate.astype(jnp.bfloat16), grad_up.astype(jnp.bfloat16)], axis=1
    )
    grad_prob = jnp.sum(hidden.astype(jnp.float32) * raw_grad, axis=1).astype(jnp.bfloat16)
    return (grad_gate_up, grad_prob)


def swap(x):
    return lax.ppermute(x, "fs", [(0, 1), (1, 0)])


def in_order(mine, theirs, first):
    return jnp.concatenate(
        [jnp.where(first, mine, theirs), jnp.where(first, theirs, mine)], axis=0
    )


def per_device_dense(tokens, cotangent, gate_probs, expert_ids, w_gate, w_up, w_down):
    tok_dev, top_count = expert_ids.shape
    experts = lax.axis_size("ep")
    width_dev = tokens.shape[1]
    hidden_units = w_gate.shape[2]
    capacity = slot_capacity(tok_dev, top_count, experts)
    slot_count = experts * capacity
    share_rows = slot_count // 2
    expert = lax.axis_index("ep")
    share = lax.axis_index("fs")
    first = share == 0
    bf16, f32 = jnp.bfloat16, jnp.float32

    packed = jnp.concatenate([expert_ids.astype(bf16), gate_probs], axis=1)
    packed_all = lax.all_gather(packed, "ep", axis=0)
    tokens_all = lax.all_gather(tokens, "ep", axis=0)
    cot_all = lax.all_gather(cotangent, "ep", axis=0)

    named = packed_all[:, :, :top_count] == expert.astype(bf16)
    chosen = jnp.any(named, axis=2)
    prob_tok = jnp.sum(
        jnp.where(named, packed_all[:, :, top_count:], jnp.zeros((), bf16)).astype(f32), axis=2
    )
    before = jnp.triu(jnp.ones((tok_dev, tok_dev), bf16), 1)
    position = jnp.dot(chosen.astype(bf16), before, preferred_element_type=f32).astype(jnp.int32)
    slot = jnp.where(chosen, position, -1)
    pick = slot[:, None, :] == jnp.arange(capacity, dtype=jnp.int32)[None, :, None]
    prob_rows = jnp.sum(jnp.where(pick, prob_tok[:, None, :], 0.0), axis=2).reshape(slot_count)
    pick = pick.astype(bf16)

    def dispatch(x):
        return (
            jnp.einsum("sct,std->scd", pick, x, preferred_element_type=f32)
            .astype(bf16)
            .reshape(slot_count, width_dev)
        )

    across_last = (((1,), (1,)), ((), ()))
    across_first = (((0,), (0,)), ((), ()))
    stacked = jnp.concatenate([w_gate[0], w_up[0]], axis=1)
    down_local = w_down[0]

    def rows_of(x, which):
        return lax.dynamic_slice_in_dim(x, which * share_rows, share_rows, 0)

    token_rows = dispatch(tokens_all)
    part_gate_up = jnp.dot(token_rows, stacked, preferred_element_type=f32).astype(bf16)
    gate_up = (
        swap(rows_of(part_gate_up, 1 - share)).astype(f32)
        + rows_of(part_gate_up, share).astype(f32)
    ).astype(bf16)
    gate_proj, up_proj, sigmoid_gate, gate_act = activate(gate_up, hidden_units)
    hidden_mine = (gate_act * up_proj).astype(bf16)
    hidden = in_order(hidden_mine, swap(hidden_mine), first)

    grad_rows = dispatch(cot_all)
    part_raw = lax.dot_general(
        grad_rows, down_local, across_last, preferred_element_type=f32
    ).astype(bf16)
    raw = swap(rows_of(part_raw, 1 - share)).astype(f32) + rows_of(part_raw, share).astype(f32)
    grads_mine, grad_prob_mine = local_grads(
        raw, gate_up, rows_of(prob_rows, share), hidden_units
    )
    grad_gate_up = in_order(grads_mine, swap(grads_mine), first)
    grad_prob = in_order(grad_prob_mine, swap(grad_prob_mine), first)

    grad_part = lax.dot_general(
        grad_gate_up, stacked, across_last, preferred_element_type=f32
    ).astype(bf16)
    dense = (
        jnp.einsum(
            "sct,scd->std",
            pick,
            grad_part.reshape(experts, capacity, width_dev),
            preferred_element_type=f32,
        )
        .astype(bf16)
        .reshape(experts * tok_dev, width_dev)
    )
    prob_dense = jnp.sum(
        pick.astype(f32) * grad_prob.reshape(experts, capacity, 1).astype(f32), axis=1
    ).astype(bf16)
    prob_dense = jnp.where(named, prob_dense[:, :, None], jnp.zeros((), bf16)).reshape(
        experts * tok_dev, top_count
    )
    grad_probs = lax.psum_scatter(prob_dense, "ep", scatter_dimension=0, tiled=True)
    grad_tokens = lax.psum_scatter(dense, "ep", scatter_dimension=0, tiled=True)

    weighted = (prob_rows[:, None] * grad_rows.astype(f32)).astype(bf16)
    new_down = lax.dot_general(
        hidden, weighted, across_first, preferred_element_type=f32
    ).astype(bf16)
    new_gate = lax.dot_general(
        token_rows, grad_gate_up[:, :hidden_units], across_first, preferred_element_type=f32
    ).astype(bf16)
    new_up = lax.dot_general(
        token_rows, grad_gate_up[:, hidden_units:], across_first, preferred_element_type=f32
    ).astype(bf16)
    return (grad_tokens, grad_probs, new_gate[None], new_up[None], new_down[None])


def slot_capacity(tok_dev, top_count, experts):
    return (9 * tok_dev * top_count + 8 * experts - 1) // (8 * experts)


def per_device(tokens, cotangent, gate_probs, expert_ids, w_gate, w_up, w_down):
    tok_dev, top_count = expert_ids.shape
    experts = lax.axis_size("ep")
    dense_rows_fit = tok_dev <= 2 * slot_capacity(tok_dev, top_count, experts)
    if lax.axis_size("fs") == 2 and experts <= 256 and dense_rows_fit:
        return per_device_dense(
            tokens, cotangent, gate_probs, expert_ids, w_gate, w_up, w_down
        )
    return per_device_slots(tokens, cotangent, gate_probs, expert_ids, w_gate, w_up, w_down)


def per_device_slots(tokens, cotangent, gate_probs, expert_ids, w_gate, w_up, w_down):
    tok_dev, top_count = expert_ids.shape
    experts = lax.axis_size("ep")
    shards = lax.axis_size("fs")
    width_dev = tokens.shape[1]
    hidden_units = w_gate.shape[2]
    capacity = slot_capacity(tok_dev, top_count, experts)
    slot_count = experts * capacity
    share_rows = slot_count // shards
    slot_of, filled_by = build_slots(expert_ids, experts, capacity)
    filled = filled_by > 0
    assign = jnp.maximum(filled_by - 1, 0)
    source_token = assign // top_count
    token_send = jnp.where(
        filled[:, None], jnp.take(tokens, source_token, axis=0), jnp.zeros((), tokens.dtype)
    ).reshape(experts, capacity, width_dev)
    grad_send = jnp.where(
        filled[:, None], jnp.take(cotangent, source_token, axis=0), jnp.zeros((), cotangent.dtype)
    ).reshape(experts, capacity, width_dev)
    prob_send = jnp.where(
        filled, jnp.take(gate_probs.reshape(-1), assign, axis=0), jnp.zeros((), gate_probs.dtype)
    ).reshape(experts, capacity)
    token_recv = lax.all_to_all(token_send, "ep", split_axis=0, concat_axis=0, tiled=True)
    token_rows = token_recv.reshape(slot_count, width_dev)
    stacked = jnp.concatenate([w_gate[0], w_up[0]], axis=1)
    down_local = w_down[0]
    section = token_rows
    summed = lax.psum(
        jnp.dot(section, stacked, preferred_element_type=jnp.float32).astype(jnp.bfloat16), "fs"
    )
    gate_up = lax.optimization_barrier(summed)
    gate_proj, up_proj, sigmoid_gate, gate_act = activate(gate_up, hidden_units)
    hidden = (gate_act * up_proj).astype(jnp.bfloat16)
    grad_recv, prob_recv = (
        lax.all_to_all(grad_send, "ep", split_axis=0, concat_axis=0, tiled=True),
        lax.all_to_all(prob_send, "ep", split_axis=0, concat_axis=0, tiled=True),
    )
    grad_rows = grad_recv.reshape(slot_count, width_dev)
    prob_rows = prob_recv.reshape(slot_count)
    weighted = (prob_rows.astype(jnp.float32)[:, None] * grad_rows.astype(jnp.float32)).astype(
        jnp.bfloat16
    )
    across_last = (((1,), (1,)), ((), ()))
    across_first = (((0,), (0,)), ((), ()))
    section = grad_rows
    raw_share = lax.psum_scatter(
        lax.dot_general(
            section, down_local, across_last, preferred_element_type=jnp.float32
        ).astype(jnp.bfloat16),
        "fs",
        scatter_dimension=0,
        tiled=True,
    ).astype(jnp.float32)
    first_row = lax.axis_index("fs") * share_rows
    share_gate_up = lax.dynamic_slice_in_dim(gate_up, first_row, share_rows, 0)
    share_prob_rows = lax.dynamic_slice_in_dim(prob_rows, first_row, share_rows, 0)
    share_grads, share_probs = local_grads(raw_share, share_gate_up, share_prob_rows, hidden_units)
    grad_gate_up, grad_prob = (
        lax.all_gather(share_grads, "fs", axis=0, tiled=True),
        lax.all_gather(share_probs, "fs", axis=0, tiled=True),
    )
    new_down = lax.dot_general(
        hidden, weighted, across_first, preferred_element_type=jnp.float32
    ).astype(jnp.bfloat16)
    joint = lax.dot_general(
        token_rows, grad_gate_up, across_first, preferred_element_type=jnp.float32
    ).astype(jnp.bfloat16)
    new_gate = joint[:, :hidden_units]
    new_up = joint[:, hidden_units:]
    grad_part = lax.dot_general(
        grad_gate_up, stacked, across_last, preferred_element_type=jnp.float32
    ).astype(jnp.bfloat16)
    part_back, prob_back = (
        lax.all_to_all(
            grad_part.reshape(experts, capacity, width_dev),
            "ep",
            split_axis=0,
            concat_axis=0,
            tiled=True,
        ),
        lax.all_to_all(
            grad_prob.reshape(experts, capacity), "ep", split_axis=0, concat_axis=0, tiled=True
        ),
    )
    returned = jnp.take(part_back.reshape(slot_count, width_dev), slot_of, axis=0)
    grad_tokens = jnp.sum(
        returned.reshape(tok_dev, top_count, width_dev).astype(jnp.float32), axis=1
    ).astype(jnp.bfloat16)
    grad_probs = jnp.take(prob_back.reshape(slot_count), slot_of, axis=0).reshape(
        tok_dev, top_count
    )
    return (grad_tokens, grad_probs, new_gate[None], new_up[None], new_down[None])


def solution(mesh):
    return jax.shard_map(
        per_device,
        mesh=mesh,
        in_specs=(
            P("ep", "fs"),
            P("ep", "fs"),
            P("ep", None),
            P("ep", None),
            P("ep", "fs", None),
            P("ep", "fs", None),
            P("ep", None, "fs"),
        ),
        out_specs=(
            P("ep", "fs"),
            P("ep", None),
            P("ep", "fs", None),
            P("ep", "fs", None),
            P("ep", None, "fs"),
        ),
        check_vma=False,
    )
```

```python
import jax
import jax.numpy as jnp
from jax import lax
from jax.experimental import pallas as pl
from jax.experimental.pallas import tpu as pltpu
from jax.sharding import PartitionSpec as P


def build_slots(routing, experts, capacity):
    flat_ids = routing.reshape(-1)
    choose = (flat_ids[:, None] == jnp.arange(experts, dtype=jnp.int32)[None, :]).astype(jnp.int32)
    earlier = jnp.cumsum(choose, axis=0) - choose
    position = jnp.sum(earlier * choose, axis=1)
    slot_of = flat_ids * capacity + position
    pair_number = jnp.arange(flat_ids.shape[0], dtype=jnp.int32) + 1
    filled_by = jnp.zeros((experts * capacity,), jnp.int32).at[slot_of].set(pair_number)
    return (slot_of, filled_by)


def activate(gate_up, hidden_units):
    gate_proj = gate_up[:, :hidden_units].astype(jnp.float32)
    up_proj = gate_up[:, hidden_units:].astype(jnp.float32)
    sigmoid_gate = jax.nn.sigmoid(gate_proj)
    gate_act = gate_proj * sigmoid_gate
    return (gate_proj, up_proj, sigmoid_gate, gate_act)


def local_grads(raw_grad, gate_up, prob_rows, hidden_units):
    gate_proj, up_proj, sigmoid_gate, gate_act = activate(gate_up, hidden_units)
    hidden = (gate_act * up_proj).astype(jnp.bfloat16)
    scaled = prob_rows.astype(jnp.float32)[:, None] * raw_grad
    grad_gate = scaled * up_proj * sigmoid_gate * (1.0 + gate_proj * (1.0 - sigmoid_gate))
    grad_up = scaled * gate_act
    grad_gate_up = jnp.concatenate(
        [grad_gate.astype(jnp.bfloat16), grad_up.astype(jnp.bfloat16)], axis=1
    )
    grad_prob = jnp.sum(hidden.astype(jnp.float32) * raw_grad, axis=1).astype(jnp.bfloat16)
    return (grad_gate_up, grad_prob)


def far_hops(count):
    return list(range(4, count, 4))


def greet(me, count):
    barrier = pltpu.get_barrier_semaphore()
    partners = [1, 2] + far_hops(count)
    for hop in partners:
        pl.semaphore_signal(
            barrier,
            inc=1,
            device_id={"ep": lax.bitwise_xor(me, hop)},
            device_id_type=pl.DeviceIdType.MESH,
        )
    pl.semaphore_wait(barrier, len(partners))


def gather_kernel(arrays, count, *refs):
    blocks, outs = refs[:arrays], refs[arrays : 2 * arrays]
    stages = refs[2 * arrays : 3 * arrays]
    send_sem, recv_sem, load_sem, store_sem = refs[3 * arrays :]
    me = lax.axis_index("ep")
    loads = [
        pltpu.make_async_copy(blocks[i], stages[i], load_sem.at[i]) for i in range(arrays)
    ]
    stores = [
        pltpu.make_async_copy(stages[i], outs[i].at[0], store_sem.at[i]) for i in range(arrays)
    ]
    for load in loads:
        load.start()
    greet(me, count)

    def send(i, source, hop):
        return pltpu.make_async_remote_copy(
            src_ref=blocks[i] if source == 0 else outs[i].at[source],
            dst_ref=outs[i].at[source + hop],
            send_sem=send_sem.at[i, source + hop],
            recv_sem=recv_sem.at[i, source + hop],
            device_id={"ep": lax.bitwise_xor(me, hop)},
            device_id_type=pl.DeviceIdType.MESH,
        )

    copies = {}

    def start(source, hop):
        for i in range(arrays):
            copies[i, source + hop] = send(i, source, hop)
            copies[i, source + hop].start()

    def arrived(slot):
        for i in range(arrays):
            copies[i, slot].wait_recv()

    far = far_hops(count)
    for hop in far:
        start(0, hop)
    start(0, 2)
    start(0, 1)
    for load, store in zip(loads, stores):
        load.wait()
        store.start()
    for slot in far:
        arrived(slot)
        start(slot, 2)
        start(slot, 1)
    for slot in [0] + far:
        arrived(slot + 2)
        start(slot + 2, 1)
    for slot in [0] + far:
        arrived(slot + 1)
        arrived(slot + 3)
    for copy in copies.values():
        copy.wait_send()
    for store in stores:
        store.wait()


def gather(collective_id, *blocks):
    count = lax.axis_size("ep")
    arrays = len(blocks)
    return pl.pallas_call(
        lambda *refs: gather_kernel(arrays, count, *refs),
        out_shape=[jax.ShapeDtypeStruct((count,) + b.shape, b.dtype) for b in blocks],
        in_specs=[pl.BlockSpec(memory_space=pl.ANY)] * arrays,
        out_specs=[pl.BlockSpec(memory_space=pl.ANY)] * arrays,
        scratch_shapes=[pltpu.VMEM(b.shape, b.dtype) for b in blocks]
        + [
            pltpu.SemaphoreType.DMA((arrays, count)),
            pltpu.SemaphoreType.DMA((arrays, count)),
            pltpu.SemaphoreType.DMA((arrays,)),
            pltpu.SemaphoreType.DMA((arrays,)),
        ],
        compiler_params=pltpu.CompilerParams(
            collective_id=collective_id, has_side_effects=True
        ),
        name=f"gather_{collective_id}",
    )(*blocks)


def swap(x):
    return lax.ppermute(x, "fs", [(0, 1), (1, 0)])


def in_order(mine, theirs, first):
    return jnp.concatenate(
        [jnp.where(first, mine, theirs), jnp.where(first, theirs, mine)], axis=0
    )


def per_device_dense(tokens, cotangent, gate_probs, expert_ids, w_gate, w_up, w_down):
    tok_dev, top_count = expert_ids.shape
    experts = lax.axis_size("ep")
    width_dev = tokens.shape[1]
    hidden_units = w_gate.shape[2]
    capacity = slot_capacity(tok_dev, top_count, experts)
    slot_count = experts * capacity
    share_rows = slot_count // 2
    expert = lax.axis_index("ep")
    share = lax.axis_index("fs")
    first = share == 0
    bf16, f32 = jnp.bfloat16, jnp.float32

    packed = jnp.concatenate([expert_ids.astype(bf16), gate_probs], axis=1)
    packed = jnp.pad(packed, ((0, 0), (0, 128 - 2 * top_count)))
    tokens_all, packed_all = gather(0, tokens, packed)

    named = packed_all[:, :, :top_count] == expert.astype(bf16)
    chosen = jnp.any(named, axis=2)
    prob_tok = jnp.sum(
        jnp.where(named, packed_all[:, :, top_count : 2 * top_count], jnp.zeros((), bf16)).astype(f32), axis=2
    )
    before = jnp.triu(jnp.ones((tok_dev, tok_dev), bf16), 1)
    position = jnp.dot(chosen.astype(bf16), before, preferred_element_type=f32).astype(jnp.int32)
    slot = jnp.where(chosen, position, -1)
    pick = slot[:, None, :] == jnp.arange(capacity, dtype=jnp.int32)[None, :, None]
    prob_rows = jnp.sum(jnp.where(pick, prob_tok[:, None, :], 0.0), axis=2).reshape(slot_count)
    pick = pick.astype(bf16)

    def dispatch(x):
        return (
            jnp.einsum("sct,std->scd", pick, x, preferred_element_type=f32)
            .astype(bf16)
            .reshape(slot_count, width_dev)
        )

    across_last = (((1,), (1,)), ((), ()))
    across_first = (((0,), (0,)), ((), ()))
    stacked = jnp.concatenate([w_gate[0], w_up[0]], axis=1)
    down_local = w_down[0]

    def rows_of(x, which):
        return lax.dynamic_slice_in_dim(x, which * share_rows, share_rows, 0)

    token_rows = dispatch(tokens_all)
    part_gate_up = jnp.dot(token_rows, stacked, preferred_element_type=f32).astype(bf16)
    part_theirs = swap(rows_of(part_gate_up, 1 - share))
    cotangent, part_gate_up = lax.optimization_barrier((cotangent, part_gate_up))
    (cot_all,) = gather(1, cotangent)
    gate_up = (
        part_theirs.astype(f32)
        + rows_of(part_gate_up, share).astype(f32)
    ).astype(bf16)
    gate_proj, up_proj, sigmoid_gate, gate_act = activate(gate_up, hidden_units)
    hidden_mine = (gate_act * up_proj).astype(bf16)
    hidden = in_order(hidden_mine, swap(hidden_mine), first)

    grad_rows = dispatch(cot_all)
    part_raw = lax.dot_general(
        grad_rows, down_local, across_last, preferred_element_type=f32
    ).astype(bf16)
    raw = swap(rows_of(part_raw, 1 - share)).astype(f32) + rows_of(part_raw, share).astype(f32)
    grads_mine, grad_prob_mine = local_grads(
        raw, gate_up, rows_of(prob_rows, share), hidden_units
    )
    grad_gate_up = in_order(grads_mine, swap(grads_mine), first)
    grad_prob = in_order(grad_prob_mine, swap(grad_prob_mine), first)

    grad_part = lax.dot_general(
        grad_gate_up, stacked, across_last, preferred_element_type=f32
    ).astype(bf16)
    dense = (
        jnp.einsum(
            "sct,scd->std",
            pick,
            grad_part.reshape(experts, capacity, width_dev),
            preferred_element_type=f32,
        )
        .astype(bf16)
        .reshape(experts * tok_dev, width_dev)
    )
    prob_dense = jnp.sum(
        pick.astype(f32) * grad_prob.reshape(experts, capacity, 1).astype(f32), axis=1
    ).astype(bf16)
    prob_dense = jnp.where(named, prob_dense[:, :, None], jnp.zeros((), bf16)).reshape(
        experts * tok_dev, top_count
    )
    source = lax.bitwise_xor(jnp.arange(experts, dtype=jnp.int32), expert)
    prob_dense = jnp.take(prob_dense.reshape(experts, tok_dev, top_count), source, axis=0)
    prob_dense = prob_dense.reshape(experts * tok_dev, top_count)
    dense = jnp.take(dense.reshape(experts, tok_dev, width_dev), source, axis=0)
    dense = dense.reshape(experts * tok_dev, width_dev)
    grad_probs = lax.psum_scatter(prob_dense, "ep", scatter_dimension=0, tiled=True)
    grad_tokens = lax.psum_scatter(dense, "ep", scatter_dimension=0, tiled=True)

    weighted = (prob_rows[:, None] * grad_rows.astype(f32)).astype(bf16)
    new_down = lax.dot_general(
        hidden, weighted, across_first, preferred_element_type=f32
    ).astype(bf16)
    new_gate = lax.dot_general(
        token_rows, grad_gate_up[:, :hidden_units], across_first, preferred_element_type=f32
    ).astype(bf16)
    new_up = lax.dot_general(
        token_rows, grad_gate_up[:, hidden_units:], across_first, preferred_element_type=f32
    ).astype(bf16)
    return (grad_tokens, grad_probs, new_gate[None], new_up[None], new_down[None])


def slot_capacity(tok_dev, top_count, experts):
    return (9 * tok_dev * top_count + 8 * experts - 1) // (8 * experts)


def per_device(tokens, cotangent, gate_probs, expert_ids, w_gate, w_up, w_down):
    tok_dev, top_count = expert_ids.shape
    experts = lax.axis_size("ep")
    dense_rows_fit = tok_dev <= 2 * slot_capacity(tok_dev, top_count, experts)
    if lax.axis_size("fs") == 2 and experts == 16 and dense_rows_fit:
        return per_device_dense(
            tokens, cotangent, gate_probs, expert_ids, w_gate, w_up, w_down
        )
    return per_device_slots(tokens, cotangent, gate_probs, expert_ids, w_gate, w_up, w_down)


def per_device_slots(tokens, cotangent, gate_probs, expert_ids, w_gate, w_up, w_down):
    tok_dev, top_count = expert_ids.shape
    experts = lax.axis_size("ep")
    shards = lax.axis_size("fs")
    width_dev = tokens.shape[1]
    hidden_units = w_gate.shape[2]
    capacity = slot_capacity(tok_dev, top_count, experts)
    slot_count = experts * capacity
    share_rows = slot_count // shards
    slot_of, filled_by = build_slots(expert_ids, experts, capacity)
    filled = filled_by > 0
    assign = jnp.maximum(filled_by - 1, 0)
    source_token = assign // top_count
    token_send = jnp.where(
        filled[:, None], jnp.take(tokens, source_token, axis=0), jnp.zeros((), tokens.dtype)
    ).reshape(experts, capacity, width_dev)
    grad_send = jnp.where(
        filled[:, None], jnp.take(cotangent, source_token, axis=0), jnp.zeros((), cotangent.dtype)
    ).reshape(experts, capacity, width_dev)
    prob_send = jnp.where(
        filled, jnp.take(gate_probs.reshape(-1), assign, axis=0), jnp.zeros((), gate_probs.dtype)
    ).reshape(experts, capacity)
    token_recv = lax.all_to_all(token_send, "ep", split_axis=0, concat_axis=0, tiled=True)
    token_rows = token_recv.reshape(slot_count, width_dev)
    stacked = jnp.concatenate([w_gate[0], w_up[0]], axis=1)
    down_local = w_down[0]
    section = token_rows
    summed = lax.psum(
        jnp.dot(section, stacked, preferred_element_type=jnp.float32).astype(jnp.bfloat16), "fs"
    )
    gate_up = lax.optimization_barrier(summed)
    gate_proj, up_proj, sigmoid_gate, gate_act = activate(gate_up, hidden_units)
    hidden = (gate_act * up_proj).astype(jnp.bfloat16)
    grad_recv, prob_recv = (
        lax.all_to_all(grad_send, "ep", split_axis=0, concat_axis=0, tiled=True),
        lax.all_to_all(prob_send, "ep", split_axis=0, concat_axis=0, tiled=True),
    )
    grad_rows = grad_recv.reshape(slot_count, width_dev)
    prob_rows = prob_recv.reshape(slot_count)
    weighted = (prob_rows.astype(jnp.float32)[:, None] * grad_rows.astype(jnp.float32)).astype(
        jnp.bfloat16
    )
    across_last = (((1,), (1,)), ((), ()))
    across_first = (((0,), (0,)), ((), ()))
    section = grad_rows
    raw_share = lax.psum_scatter(
        lax.dot_general(
            section, down_local, across_last, preferred_element_type=jnp.float32
        ).astype(jnp.bfloat16),
        "fs",
        scatter_dimension=0,
        tiled=True,
    ).astype(jnp.float32)
    first_row = lax.axis_index("fs") * share_rows
    share_gate_up = lax.dynamic_slice_in_dim(gate_up, first_row, share_rows, 0)
    share_prob_rows = lax.dynamic_slice_in_dim(prob_rows, first_row, share_rows, 0)
    share_grads, share_probs = local_grads(raw_share, share_gate_up, share_prob_rows, hidden_units)
    grad_gate_up, grad_prob = (
        lax.all_gather(share_grads, "fs", axis=0, tiled=True),
        lax.all_gather(share_probs, "fs", axis=0, tiled=True),
    )
    new_down = lax.dot_general(
        hidden, weighted, across_first, preferred_element_type=jnp.float32
    ).astype(jnp.bfloat16)
    joint = lax.dot_general(
        token_rows, grad_gate_up, across_first, preferred_element_type=jnp.float32
    ).astype(jnp.bfloat16)
    new_gate = joint[:, :hidden_units]
    new_up = joint[:, hidden_units:]
    grad_part = lax.dot_general(
        grad_gate_up, stacked, across_last, preferred_element_type=jnp.float32
    ).astype(jnp.bfloat16)
    part_back, prob_back = (
        lax.all_to_all(
            grad_part.reshape(experts, capacity, width_dev),
            "ep",
            split_axis=0,
            concat_axis=0,
            tiled=True,
        ),
        lax.all_to_all(
            grad_prob.reshape(experts, capacity), "ep", split_axis=0, concat_axis=0, tiled=True
        ),
    )
    returned = jnp.take(part_back.reshape(slot_count, width_dev), slot_of, axis=0)
    grad_tokens = jnp.sum(
        returned.reshape(tok_dev, top_count, width_dev).astype(jnp.float32), axis=1
    ).astype(jnp.bfloat16)
    grad_probs = jnp.take(prob_back.reshape(slot_count), slot_of, axis=0).reshape(
        tok_dev, top_count
    )
    return (grad_tokens, grad_probs, new_gate[None], new_up[None], new_down[None])


def solution(mesh):
    return jax.shard_map(
        per_device,
        mesh=mesh,
        in_specs=(
            P("ep", "fs"),
            P("ep", "fs"),
            P("ep", None),
            P("ep", None),
            P("ep", "fs", None),
            P("ep", "fs", None),
            P("ep", None, "fs"),
        ),
        out_specs=(
            P("ep", "fs"),
            P("ep", None),
            P("ep", "fs", None),
            P("ep", "fs", None),
            P("ep", None, "fs"),
        ),
        check_vma=False,
    )
```
